32 devices in a mesh: prow: 8 (over z, y), pcol: 4 (over x, core).
Axes of the slice: x: 2, y: 2, z: 4, core: 2. Of those that a mesh axis runs over, the one named last changes fastest.
Arguments:
- paper_x: bfloat16 [8192, 768], P(('prow', 'pcol')), may hold values from -6 to 6
- author_x: bfloat16 [4096, 768], P(('pcol', 'prow')), may hold values from -6 to 6
- w_self: bfloat16 [768, 768], replicated, may hold values from -0.21875 to 0.21875
- w_rel: bfloat16 [2, 768, 768], replicated, may hold values from -0.009765625 to 0.009765625
- w_two: bfloat16 [768, 768], replicated, may hold values from -0.0068359375 to 0.0068359375
- block_rows: int32 [8, 4, 32], P('prow', 'pcol'), may hold values from 0 to 7, as said below
- block_cols: int32 [8, 4, 32], P('prow', 'pcol'), may hold values from 0 to 7, as said below
- block_type: int32 [8, 4, 32], P('prow', 'pcol'), may hold values from 0 to 1
- block_count: int32 [8, 4], P('prow', 'pcol'), may hold values from 8 to 32, as said below
- block_vals: bfloat16 [8, 4, 32, 128, 128], P('prow', 'pcol'), may hold values from 0 to 1, as said below
Outputs:
- paper_hidden: bfloat16 [8192, 768], P(('prow', 'pcol'))
- author_out: bfloat16 [4096, 768], P(('pcol', 'prow'))
The draws below stay inside these ranges and needn't reach their ends.
Inputs may be any that keep to these rules, and one draw needn't show every extreme that they name: `block_rows`: within one tile the live and dead slots name distinct positions; block rows are below 8. `block_cols`: block columns are below 8; with block_rows, positions of one tile are distinct. `block_count`: slots 0 to count - 1 of a tile are live; some tile holds 32 live slots and some tile 32 // 4 in every draw. `block_vals`: every entry is 0 or 1.
All inputs are finite; a program needn't handle non-finite values.
Results may differ from the reference program's by a relative error of at most 0.0041.
Values may be sent and summed in bfloat16 or wider, within the bound.
A program may use at most 64 MiB of HBM per device.

```python
import jax
import jax.numpy as jnp
from jax import lax

WIDTH = 768
BLOCK = 128
RELATIONS = 2
ROW_BLOCKS = 8
COL_BLOCKS = 8
SLOTS = 32
PAPERS = 8192
AUTHORS = 4096
N_PROW = 8
N_PCOL = 4


def tile_positions(key):
    keys = jax.random.split(jax.random.fold_in(key, 7), N_PROW * N_PCOL)
    chosen = jax.vmap(lambda single: jax.random.permutation(single, ROW_BLOCKS * COL_BLOCKS)[:SLOTS])(keys)
    return chosen.reshape(N_PROW, N_PCOL, SLOTS).astype(jnp.int32)


def draw_block_rows(key, part):
    return (tile_positions(key) // COL_BLOCKS).astype(jnp.int32)


def draw_block_cols(key, part):
    return (tile_positions(key) % COL_BLOCKS).astype(jnp.int32)


def draw_block_count(key, part):
    tiles = N_PROW * N_PCOL
    counts = jax.random.randint(jax.random.fold_in(key, 11), (tiles,), SLOTS // 4, SLOTS + 1)
    fullest = jax.random.randint(jax.random.fold_in(key, 12), (), 0, tiles)
    offset = jax.random.randint(jax.random.fold_in(key, 13), (), 0, tiles - 1)
    emptiest = (fullest + 1 + offset) % tiles
    places = jnp.arange(tiles, dtype=jnp.int32)
    counts = jnp.where(places == fullest, SLOTS, counts)
    counts = jnp.where(places == emptiest, SLOTS // 4, counts)
    return counts.reshape(N_PROW, N_PCOL).astype(jnp.int32)


def draw_block_vals(key, part):
    shape = (N_PROW, N_PCOL, SLOTS, BLOCK, BLOCK)
    ones = jax.random.bernoulli(jax.random.fold_in(key, 17), 0.5, shape).astype(jnp.float32)
    return ones.astype(jnp.bfloat16)


def with_ends(array, rng, least, largest):
    index_at = [jax.random.randint(jax.random.fold_in(rng, axis), (), 0, length) for axis, length in enumerate(array.shape)]
    main_axis = array.shape.index(max(array.shape))
    next_to = index_at[:main_axis] + [(index_at[main_axis] + 1) % array.shape[main_axis]] + index_at[main_axis + 1:]
    return array.at[tuple(index_at)].set(least).at[tuple(next_to)].set(largest)


def shard_levels(rng, dims, cuts, least, high):
    level = 1.0
    for position, shards_of in cuts:
        steps = jax.random.uniform(jax.random.fold_in(jax.random.fold_in(rng, 6), position), (shards_of,), jnp.float32, least / len(cuts), high / len(cuts))
        level = level * jnp.repeat(jnp.exp(steps), dims[position] // shards_of).reshape((-1,) + (1,) * (len(dims) - 1 - position))
    return level


def scatter_about(key, dims, width, most, cuts=(), kind=jnp.bfloat16):
    array = jax.random.normal(key, dims, jnp.float32) * width
    if len(cuts) > 0:
        array = shard_levels(key, dims, cuts, -0.22, 0.18) * array
    return jnp.clip(array, min=-most, max=most).astype(kind)


def setup_inputs(seed: int = 0) -> dict:
    arg_keys = jax.random.split(jax.random.key(seed), 11)
    return {
        "paper_x": scatter_about(arg_keys[0], (PAPERS, WIDTH), 1.0, 6.0, ((0, 32),)),
        "author_x": scatter_about(arg_keys[1], (AUTHORS, WIDTH), 1.0, 6.0, ((0, 32),)),
        "w_self": scatter_about(arg_keys[2], (WIDTH, WIDTH), WIDTH ** -0.5, 0.21875),
        "w_rel": scatter_about(arg_keys[3], (RELATIONS, WIDTH, WIDTH), (WIDTH * (BLOCK // 4) * SLOTS * N_PCOL // ROW_BLOCKS) ** -0.5, 0.009765625),
        "w_two": scatter_about(arg_keys[4], (WIDTH, WIDTH), (WIDTH * (BLOCK // 4) * SLOTS * N_PROW // COL_BLOCKS) ** -0.5, 0.0068359375),
        "block_rows": draw_block_rows(jax.random.fold_in(arg_keys[10], 71), 0),
        "block_cols": draw_block_cols(jax.random.fold_in(arg_keys[10], 71), 0),
        "block_type": with_ends(jax.random.randint(arg_keys[7], (N_PROW, N_PCOL, SLOTS), 0, RELATIONS), jax.random.fold_in(arg_keys[7], 1), 0, RELATIONS - 1).astype(jnp.int32),
        "block_count": draw_block_count(jax.random.fold_in(arg_keys[10], 71), 0),
        "block_vals": draw_block_vals(jax.random.fold_in(arg_keys[10], 71), 0),
    }


def reference(paper_x, author_x, w_self, w_rel, w_two, block_rows, block_cols, block_type, block_count, block_vals):
    paper_blocks = PAPERS // BLOCK
    author_blocks = AUTHORS // BLOCK
    tiles = N_PROW * N_PCOL
    messages = jnp.stack([jnp.dot(author_x, w_rel[index], preferred_element_type=jnp.float32) for index in range(RELATIONS)]).astype(jnp.bfloat16)
    grid_row = (jnp.arange(N_PROW, dtype=jnp.int32)[:, None, None] * ROW_BLOCKS + block_rows).reshape(tiles, SLOTS).astype(jnp.int32)
    grid_col = (jnp.arange(N_PCOL, dtype=jnp.int32)[None, :, None] * COL_BLOCKS + block_cols).reshape(tiles, SLOTS).astype(jnp.int32)
    type_ids = block_type.reshape(tiles, SLOTS)
    live = (jnp.arange(SLOTS, dtype=jnp.int32)[None, None, :] < block_count[:, :, None]).astype(jnp.float32).reshape(tiles, SLOTS)
    contents = block_vals.reshape(tiles, SLOTS, BLOCK, BLOCK)
    table = messages.reshape(RELATIONS * author_blocks, BLOCK, WIDTH)

    def first_hop(total, item):
        rows_now, cols_now, types_now, mask_now, content_now = item
        picked = table[(types_now * author_blocks + cols_now).astype(jnp.int32)]
        product = jnp.einsum("kpa,kaf->kpf", content_now.astype(jnp.float32), picked.astype(jnp.float32))
        return total.at[rows_now].add(product * mask_now[:, None, None]), None

    start = jnp.zeros((paper_blocks, BLOCK, WIDTH), jnp.float32)
    gathered, _ = lax.scan(first_hop, start, (grid_row, grid_col, type_ids, live, contents))
    gathered = gathered.reshape(PAPERS, WIDTH)
    self_term = jnp.dot(paper_x, w_self, preferred_element_type=jnp.float32)
    paper_hidden = jnp.maximum(self_term + gathered, 0.0).astype(jnp.bfloat16)
    outgoing = jnp.dot(paper_hidden, w_two, preferred_element_type=jnp.float32).astype(jnp.bfloat16)
    paper_table = outgoing.reshape(paper_blocks, BLOCK, WIDTH)

    def second_hop(total, item):
        rows_now, cols_now, mask_now, content_now = item
        picked = paper_table[rows_now]
        product = jnp.einsum("kpa,kpf->kaf", content_now.astype(jnp.float32), picked.astype(jnp.float32))
        return total.at[cols_now].add(product * mask_now[:, None, None]), None

    start_two = jnp.zeros((author_blocks, BLOCK, WIDTH), jnp.float32)
    author_total, _ = lax.scan(second_hop, start_two, (grid_row, grid_col, live, contents))
    author_out = author_total.reshape(AUTHORS, WIDTH).astype(jnp.bfloat16)
    return paper_hidden, author_out
```

```python
import functools

import jax
import jax.numpy as jnp
from jax import lax
from jax.experimental import pallas as pl
from jax.experimental.pallas import tpu as pltpu
from jax.sharding import PartitionSpec as P

MESH = pl.DeviceIdType.MESH
F32 = jnp.float32
BF16 = jnp.bfloat16


def dot(a, b):
    return jnp.dot(a, b, preferred_element_type=F32)


def kernel(
    n_prow, n_pcol, tile,
    tab, author, paper_h, w_self_h, w_rel_h, w_two_h, blocks_h,
    hidden, author_out,
    paper, w_self, w_rel, w_two, blocks,
    x_all, msgs, dense, dense_t, self_term,
    pair_out, pair_in, x_out, x_in, acc,
    rows_all, y_out, y_in, y_acc, z_out, z_in,
    local_sem,
    g_send, g_recv, gy_send, gy_recv,
    pair_s, pair_r, xs, xr,
    o_send, o_recv, oc_send, oc_recv,
    ys, yr, zs, zr,
):
    i = lax.axis_index("prow")
    j = lax.axis_index("pcol")
    z, y = i // 2, i % 2
    x, c = j // 2, j % 2
    H, G = n_prow // 2, n_pcol // 2
    own_papers, width = paper.shape
    own_authors = author.shape[0]
    side = blocks.shape[1]
    authors = own_authors * n_prow
    papers = own_papers * n_pcol
    nf = width // tile
    y_part = z * 2 + 1 - y
    c_part = x * 2 + 1 - c

    waits = []

    def send(cond, src, dst, ss, rs, di, dj):
        def desc():
            return pltpu.make_async_remote_copy(
                src_ref=src, dst_ref=dst, send_sem=ss, recv_sem=rs,
                device_id=(di, dj), device_id_type=MESH,
            )

        if cond is None:
            desc().start()
        else:
            @pl.when(cond)
            def _():
                desc().start()
        waits.append((cond, desc))

    def arrive(dst, ss, rs):
        pltpu.make_async_remote_copy(
            src_ref=dst, dst_ref=dst, send_sem=ss, recv_sem=rs,
            device_id=(i, c_part), device_id_type=MESH,
        ).wait_recv()

    loads = [
        pltpu.make_async_copy(src, dst, local_sem.at[n])
        for n, (src, dst) in enumerate(
            ((blocks_h, blocks), (w_rel_h, w_rel), (paper_h, paper), (w_self_h, w_self), (w_two_h, w_two))
        )
    ]
    for load in loads:
        load.start()

    barrier = pltpu.get_barrier_semaphore()

    def greet(cond, di, dj):
        def go():
            pl.semaphore_signal(barrier, inc=1, device_id=(di, dj), device_id_type=MESH)

        if cond is None:
            go()
        else:
            pl.when(cond)(go)

    up_z, down_z, up_x, down_x = z < H - 1, z > 0, x < G - 1, x > 0
    greet(None, y_part, j)
    greet(None, i, c_part)
    greet(up_z, i + 2, j)
    greet(down_z, i - 2, j)
    greet(up_x, i, j + 2)
    greet(down_x, i, j - 2)
    peers = 2
    for cond in (up_z, down_z, up_x, down_x):
        peers = peers + cond.astype(jnp.int32)
    pl.semaphore_wait(barrier, peers)

    send(up_z, author, x_all.at[z, y], g_send.at[0, 0], g_recv.at[0, 0], i + 2, j)
    send(down_z, author, x_all.at[z, y], g_send.at[1, 0], g_recv.at[1, 0], i - 2, j)
    send(None, author, x_all.at[z, y], gy_send.at[2, 0], gy_recv.at[2, 0], y_part, j)
    x_all[z, y] = author[...]

    loads[0].wait()
    row_blocks, col_blocks = papers // side, authors // side
    p_step, a_step = min(side, own_papers), min(side, own_authors)
    for rb in range(row_blocks):
        for cb in range(col_blocks):
            pos = rb * col_blocks + cb
            slot, kind = tab[0, pos], tab[1, pos]
            block = blocks[slot].astype(F32)
            for t in range(2):
                part = (block * (kind == t).astype(F32)).astype(BF16)
                lo = t * authors + cb * side
                for sub in range(side // p_step):
                    row = rb * side + sub * p_step
                    dense[row // own_papers, row % own_papers:row % own_papers + p_step, lo:lo + side] = part[
                        sub * p_step:(sub + 1) * p_step
                    ]
            flip = (block * (kind < 2).astype(F32)).T.astype(BF16)
            for sub in range(side // a_step):
                owner = (cb * side + sub * a_step) // own_authors
                dense_t[owner % 2, owner // 2, :, rb * side:(rb + 1) * side] = flip[sub * a_step:(sub + 1) * a_step]

    loads[2].wait()
    loads[3].wait()
    for f in range(nf):
        cols = slice(f * tile, (f + 1) * tile)
        self_term[:, cols] = dot(paper[...], w_self[:, cols])
    loads[1].wait()
    loads[4].wait()

    def message_pair(zz):
        pair = x_all[zz].reshape(2 * own_authors, width)
        for t in range(2):
            @pl.loop(0, nf)
            def _(n):
                cols = pl.ds(pl.multiple_of(n * tile, tile), tile)
                msgs[t, zz, :, cols] = dot(pair, w_rel[t, :, cols]).astype(BF16)

    def z_arrival(s):
        below, above = z - 1 - s, z + 1 + s

        @pl.when(below >= 0)
        def _():
            arrive(x_all.at[below, y], g_send.at[0, s], g_recv.at[0, s])

        if s + 1 <= H - 2:
            send((below >= 0) & up_z, x_all.at[below, y], x_all.at[below, y],
                 g_send.at[0, s + 1], g_recv.at[0, s + 1], i + 2, j)
        send(below >= 0, x_all.at[below, y], x_all.at[below, y], gy_send.at[0, s], gy_recv.at[0, s], y_part, j)

        @pl.when(above <= H - 1)
        def _():
            arrive(x_all.at[above, y], g_send.at[1, s], g_recv.at[1, s])

        if s + 1 <= H - 2:
            send((above <= H - 1) & down_z, x_all.at[above, y], x_all.at[above, y],
                 g_send.at[1, s + 1], g_recv.at[1, s + 1], i - 2, j)
        send(above <= H - 1, x_all.at[above, y], x_all.at[above, y], gy_send.at[1, s], gy_recv.at[1, s], y_part, j)

    def y_arrival(s):
        below, above = z - 1 - s, z + 1 + s

        @pl.when(below >= 0)
        def _():
            arrive(x_all.at[below, 1 - y], gy_send.at[0, s], gy_recv.at[0, s])
            message_pair(below)

        @pl.when(above <= H - 1)
        def _():
            arrive(x_all.at[above, 1 - y], gy_send.at[1, s], gy_recv.at[1, s])
            message_pair(above)

    for s in range(H - 1):
        z_arrival(s)
        if s == 0:
            arrive(x_all.at[z, 1 - y], gy_send.at[2, 0], gy_recv.at[2, 0])
            message_pair(z)
        else:
            y_arrival(s - 1)
    y_arrival(H - 2)

    def first_hop(q, f):
        cols = slice(f * tile, (f + 1) * tile)
        return dot(dense[q], msgs[:, :, :, cols].reshape(2 * authors, tile))

    for d in range(1, G + 1):
        b = lax.rem(x + d, G)
        for f in range(nf):
            pair_out[d - 1, f] = first_hop(b * 2 + 1 - c, f).astype(BF16)
            send(None, pair_out.at[d - 1, f], pair_in.at[d - 1, f], pair_s.at[d - 1, f], pair_r.at[d - 1, f], i, c_part)
        for f in range(nf):
            acc[f] = first_hop(b * 2 + c, f)
            arrive(pair_in.at[d - 1, f], pair_s.at[d - 1, f], pair_r.at[d - 1, f])
            acc[f] = acc[f] + pair_in[d - 1, f].astype(F32)
            if d == G:
                continue
            is_up, is_down = b > x, b < x

            @pl.when(is_up & (x > 0))
            def _():
                arrive(x_in.at[0, b, f], xs.at[0, b, f], xr.at[0, b, f])
                acc[f] = acc[f] + x_in[0, b, f].astype(F32)

            @pl.when(is_down & (x < G - 1))
            def _():
                arrive(x_in.at[1, b, f], xs.at[1, b, f], xr.at[1, b, f])
                acc[f] = acc[f] + x_in[1, b, f].astype(F32)

            x_out[d - 1, f] = acc[f].astype(BF16)
            send(is_up, x_out.at[d - 1, f], x_in.at[0, b, f], xs.at[0, b, f], xr.at[0, b, f], i, j + 2)
            send(is_down, x_out.at[d - 1, f], x_in.at[1, b, f], xs.at[1, b, f], xr.at[1, b, f], i, j - 2)

    for f in range(nf):
        cols = slice(f * tile, (f + 1) * tile)

        @pl.when(x > 0)
        def _():
            arrive(x_in.at[0, x, f], xs.at[0, x, f], xr.at[0, x, f])
            acc[f] = acc[f] + x_in[0, x, f].astype(F32)

        @pl.when(x < G - 1)
        def _():
            arrive(x_in.at[1, x, f], xs.at[1, x, f], xr.at[1, x, f])
            acc[f] = acc[f] + x_in[1, x, f].astype(F32)

        hidden[:, cols] = jnp.maximum(acc[f] + self_term[:, cols], 0.0).astype(BF16)

    for f in range(nf):
        cols = slice(f * tile, (f + 1) * tile)
        rows_all[f, x, c] = dot(hidden[...], w_two[:, cols]).astype(BF16)
        own = rows_all.at[f, x, c]
        send(up_x, own, own, o_send.at[0, 0, f], o_recv.at[0, 0, f], i, j + 2)
        send(down_x, own, own, o_send.at[1, 0, f], o_recv.at[1, 0, f], i, j - 2)
        send(None, own, own, oc_send.at[2, 0, f], oc_recv.at[2, 0, f], i, c_part)

    def pass_on(f):
        for s in range(G - 1):
            below, above = x - 1 - s, x + 1 + s

            @pl.when(below >= 0)
            def _():
                arrive(rows_all.at[f, below, c], o_send.at[0, s, f], o_recv.at[0, s, f])

            part = rows_all.at[f, below, c]
            if s + 1 <= G - 2:
                send((below >= 0) & up_x, part, part, o_send.at[0, s + 1, f], o_recv.at[0, s + 1, f], i, j + 2)
            send(below >= 0, part, part, oc_send.at[0, s, f], oc_recv.at[0, s, f], i, c_part)

            @pl.when(above <= G - 1)
            def _():
                arrive(rows_all.at[f, above, c], o_send.at[1, s, f], o_recv.at[1, s, f])

            part = rows_all.at[f, above, c]
            if s + 1 <= G - 2:
                send((above <= G - 1) & down_x, part, part, o_send.at[1, s + 1, f], o_recv.at[1, s + 1, f], i, j - 2)
            send(above <= G - 1, part, part, oc_send.at[1, s, f], oc_recv.at[1, s, f], i, c_part)

    def collect(f):
        arrive(rows_all.at[f, x, 1 - c], oc_send.at[2, 0, f], oc_recv.at[2, 0, f])
        for s in range(G - 1):
            below, above = x - 1 - s, x + 1 + s

            @pl.when(below >= 0)
            def _():
                arrive(rows_all.at[f, below, 1 - c], oc_send.at[0, s, f], oc_recv.at[0, s, f])

            @pl.when(above <= G - 1)
            def _():
                arrive(rows_all.at[f, above, 1 - c], oc_send.at[1, s, f], oc_recv.at[1, s, f])

    for f in range(nf):
        pass_on(f)
        collect(f)
        table = rows_all[f].reshape(papers, tile)
        far = dot(dense_t[1 - y].reshape(H * own_authors, papers), table)
        y_out[f] = far.astype(BF16).reshape(H, own_authors, tile)
        send(None, y_out.at[f], y_in.at[f], ys.at[f], yr.at[f], y_part, j)
        near = dot(dense_t[y].reshape(H * own_authors, papers), table)
        y_acc[f] = near.reshape(H, own_authors, tile)

    for f in range(nf):
        arrive(y_in.at[f], ys.at[f], yr.at[f])
        y_acc[f] = y_acc[f] + y_in[f].astype(F32)
        for s in range(H - 1):
            for way, b in ((0, H - 1 - s), (1, s)):
                cond = (z < b) if way == 0 else (z > b)
                first = (z == 0) if way == 0 else (z == H - 1)

                @pl.when(cond & first)
                def _():
                    z_out[way, f, b] = y_acc[f, b].astype(BF16)

                @pl.when(cond & jnp.logical_not(first))
                def _():
                    arrive(z_in.at[way, f, b], zs.at[way, f, b], zr.at[way, f, b])
                    z_out[way, f, b] = (y_acc[f, b] + z_in[way, f, b].astype(F32)).astype(BF16)

                send(cond, z_out.at[way, f, b], z_in.at[way, f, b], zs.at[way, f, b], zr.at[way, f, b],
                     i + 2 if way == 0 else i - 2, j)

    for f in range(nf):
        cols = slice(f * tile, (f + 1) * tile)
        total = y_acc.at[f, z]

        @pl.when(z > 0)
        def _():
            arrive(z_in.at[0, f, z], zs.at[0, f, z], zr.at[0, f, z])
            total[...] = total[...] + z_in[0, f, z].astype(F32)

        @pl.when(z < H - 1)
        def _():
            arrive(z_in.at[1, f, z], zs.at[1, f, z], zr.at[1, f, z])
            total[...] = total[...] + z_in[1, f, z].astype(F32)

        author_out[:, cols] = total[...].astype(BF16)

    for cond, desc in waits:
        if cond is None:
            desc().wait_send()
        else:
            @pl.when(cond)
            def _():
                desc().wait_send()


def per_device(
    n_prow, n_pcol, paper_x, author_x, w_self, w_rel, w_two,
    block_rows, block_cols, block_type, block_count, block_vals,
):
    slots, side = block_vals.shape[2], block_vals.shape[3]
    own_papers, width = paper_x.shape
    own_authors = author_x.shape[0]
    papers, authors = own_papers * n_pcol, own_authors * n_prow
    col_blocks = authors // side
    places = (papers // side) * col_blocks
    H, G = n_prow // 2, n_pcol // 2
    tile = 256 if width % 256 == 0 else 128
    nf = width // tile

    slot = jnp.arange(slots, dtype=jnp.int32)
    where = block_rows.reshape(slots) * col_blocks + block_cols.reshape(slots)
    live = slot < block_count.reshape(())
    hit = (where[:, None] == jnp.arange(places, dtype=jnp.int32)[None, :]) & live[:, None]
    which = jnp.sum(jnp.where(hit, slot[:, None], 0), axis=0)
    kind = 2 + jnp.sum(jnp.where(hit, block_type.reshape(slots)[:, None] - 2, 0), axis=0)
    tab = jnp.stack([which, kind]).astype(jnp.int32)

    vmem, anyspace, smem = pltpu.VMEM, pl.ANY, pltpu.SMEM
    dma = pltpu.SemaphoreType.DMA
    hz, gx = max(H - 1, 1), max(G - 1, 1)
    return pl.pallas_call(
        functools.partial(kernel, n_prow, n_pcol, tile),
        out_shape=(
            jax.ShapeDtypeStruct((own_papers, width), BF16),
            jax.ShapeDtypeStruct((own_authors, width), BF16),
        ),
        in_specs=[pl.BlockSpec(memory_space=smem), pl.BlockSpec(memory_space=vmem)]
        + [pl.BlockSpec(memory_space=anyspace)] * 5,
        out_specs=(pl.BlockSpec(memory_space=vmem),) * 2,
        scratch_shapes=[
            vmem((own_papers, width), BF16),
            vmem((width, width), BF16),
            vmem(w_rel.shape, BF16),
            vmem((width, width), BF16),
            vmem((slots, side, side), BF16),
            vmem((H, 2, own_authors, width), BF16),
            vmem((2, H, 2 * own_authors, width), BF16),
            vmem((n_pcol, own_papers, 2 * authors), BF16),
            vmem((2, H, own_authors, papers), BF16),
            vmem((own_papers, width), F32),
            vmem((G, nf, own_papers, tile), BF16),
            vmem((G, nf, own_papers, tile), BF16),
            vmem((gx, nf, own_papers, tile), BF16),
            vmem((2, G, nf, own_papers, tile), BF16),
            vmem((nf, own_papers, tile), F32),
            vmem((nf, G, 2, own_papers, tile), BF16),
            vmem((nf, H, own_authors, tile), BF16),
            vmem((nf, H, own_authors, tile), BF16),
            vmem((nf, H, own_authors, tile), F32),
            vmem((2, nf, H, own_authors, tile), BF16),
            vmem((2, nf, H, own_authors, tile), BF16),
            dma((5,)),
            dma((2, hz)), dma((2, hz)), dma((3, hz)), dma((3, hz)),
            dma((G, nf)), dma((G, nf)), dma((2, G, nf)), dma((2, G, nf)),
            dma((2, gx, nf)), dma((2, gx, nf)), dma((3, gx, nf)), dma((3, gx, nf)),
            dma((nf,)), dma((nf,)), dma((2, nf, H)), dma((2, nf, H)),
        ],
        compiler_params=pltpu.CompilerParams(
            collective_id=0, has_side_effects=True, vmem_limit_bytes=60 * 1024 * 1024
        ),
    )(tab, author_x, paper_x, w_self, w_rel, w_two, block_vals.reshape(slots, side, side))


def solution(mesh):
    return jax.shard_map(
        functools.partial(per_device, mesh.shape["prow"], mesh.shape["pcol"]),
        mesh=mesh,
        in_specs=(
            P(("prow", "pcol"), None),
            P(("pcol", "prow"), None),
            P(),
            P(),
            P(),
            P("prow", "pcol", None),
            P("prow", "pcol", None),
            P("prow", "pcol", None),
            P("prow", "pcol"),
            P("prow", "pcol", None, None, None),
        ),
        out_specs=(P(("prow", "pcol"), None), P(("pcol", "prow"), None)),
        check_vma=False,
    )
```

```python
import functools

import jax
import jax.numpy as jnp
from jax import lax
from jax.experimental import pallas as pl
from jax.experimental.pallas import tpu as pltpu
from jax.sharding import PartitionSpec as P

MESH = pl.DeviceIdType.MESH
F32 = jnp.float32
BF16 = jnp.bfloat16


def dot(a, b):
    return jnp.dot(a, b, preferred_element_type=F32)


def kernel(
    n_prow, n_pcol, tile,
    tab, author, paper_h, w_self_h, w_rel_h, w_two_h, blocks_h,
    hidden, author_out,
    paper, w_self, w_rel, w_two, blocks,
    x_all, msgs, dense, dense_t, self_term,
    pair_out, pair_in, x_out, x_in, acc,
    rows_all, y_out, y_in, y_acc, z_out, z_in,
    local_sem,
    g_send, g_recv, gy_send, gy_recv,
    pair_s, pair_r, xs, xr,
    o_send, o_recv, oc_send, oc_recv,
    ys, yr, zs, zr,
):
    i = lax.axis_index("prow")
    j = lax.axis_index("pcol")
    z, y = i // 2, i % 2
    x, c = j // 2, j % 2
    H, G = n_prow // 2, n_pcol // 2
    own_papers, width = paper.shape
    own_authors = author.shape[0]
    side = blocks.shape[1]
    authors = own_authors * n_prow
    papers = own_papers * n_pcol
    nf = width // tile
    y_part = z * 2 + 1 - y
    c_part = x * 2 + 1 - c

    waits = []

    def send(cond, src, dst, ss, rs, di, dj):
        def desc():
            return pltpu.make_async_remote_copy(
                src_ref=src, dst_ref=dst, send_sem=ss, recv_sem=rs,
                device_id=(di, dj), device_id_type=MESH,
            )

        if cond is None:
            desc().start()
        else:
            @pl.when(cond)
            def _():
                desc().start()
        waits.append((cond, desc))

    def arrive(dst, ss, rs):
        pltpu.make_async_remote_copy(
            src_ref=dst, dst_ref=dst, send_sem=ss, recv_sem=rs,
            device_id=(i, c_part), device_id_type=MESH,
        ).wait_recv()

    loads = [
        pltpu.make_async_copy(src, dst, local_sem.at[n])
        for n, (src, dst) in enumerate(
            ((blocks_h, blocks), (w_rel_h, w_rel), (paper_h, paper), (w_self_h, w_self), (w_two_h, w_two))
        )
    ]
    for load in loads:
        load.start()

    barrier = pltpu.get_barrier_semaphore()

    def greet(cond, di, dj):
        def go():
            pl.semaphore_signal(barrier, inc=1, device_id=(di, dj), device_id_type=MESH)

        if cond is None:
            go()
        else:
            pl.when(cond)(go)

    up_z, down_z, up_x, down_x = z < H - 1, z > 0, x < G - 1, x > 0
    greet(None, y_part, j)
    greet(None, i, c_part)
    greet(up_z, i + 2, j)
    greet(down_z, i - 2, j)
    greet(up_x, i, j + 2)
    greet(down_x, i, j - 2)
    peers = 2
    for cond in (up_z, down_z, up_x, down_x):
        peers = peers + cond.astype(jnp.int32)
    pl.semaphore_wait(barrier, peers)

    parts = g_send.shape[2]
    part_rows = own_authors // parts

    def piece(zz, yy, h):
        return x_all.at[zz, yy, pl.ds(h * part_rows, part_rows), :]

    for h in range(parts):
        mine = author.at[pl.ds(h * part_rows, part_rows), :]
        send(up_z, mine, piece(z, y, h), g_send.at[0, 0, h], g_recv.at[0, 0, h], i + 2, j)
        send(down_z, mine, piece(z, y, h), g_send.at[1, 0, h], g_recv.at[1, 0, h], i - 2, j)
        send(None, mine, piece(z, y, h), gy_send.at[2, 0, h], gy_recv.at[2, 0, h], y_part, j)
    x_all[z, y] = author[...]

    loads[0].wait()
    row_blocks, col_blocks = papers // side, authors // side
    p_step, a_step = min(side, own_papers), min(side, own_authors)

    def densify(first, last):
        for rb in range(first, last):
            for cb in range(col_blocks):
                pos = rb * col_blocks + cb
                slot, kind = tab[0, pos], tab[1, pos]
                block = blocks[slot].astype(F32)
                for t in range(2):
                    part = (block * (kind == t).astype(F32)).astype(BF16)
                    lo = t * authors + cb * side
                    for sub in range(side // p_step):
                        row = rb * side + sub * p_step
                        dense[row // own_papers, row % own_papers:row % own_papers + p_step, lo:lo + side] = part[
                            sub * p_step:(sub + 1) * p_step
                        ]
                flip = (block * (kind < 2).astype(F32)).T.astype(BF16)
                for sub in range(side // a_step):
                    owner = (cb * side + sub * a_step) // own_authors
                    dense_t[owner % 2, owner // 2, :, rb * side:(rb + 1) * side] = flip[sub * a_step:(sub + 1) * a_step]

    def message_pair(zz):
        pair = x_all[zz].reshape(2 * own_authors, width)
        for t in range(2):
            @pl.loop(0, nf)
            def _(n):
                cols = pl.ds(pl.multiple_of(n * tile, tile), tile)
                msgs[t, zz, :, cols] = dot(pair, w_rel[t, :, cols]).astype(BF16)

    def z_arrival(s):
        for h in range(parts):
            for way, near, inside, more, to in (
                (0, z - 1 - s, z - 1 - s >= 0, up_z, i + 2),
                (1, z + 1 + s, z + 1 + s <= H - 1, down_z, i - 2),
            ):
                part = piece(near, y, h)

                @pl.when(inside)
                def _():
                    arrive(part, g_send.at[way, s, h], g_recv.at[way, s, h])

                if s + 1 <= H - 2:
                    send(inside & more, part, part, g_send.at[way, s + 1, h], g_recv.at[way, s + 1, h], to, j)
                send(inside, part, part, gy_send.at[way, s, h], gy_recv.at[way, s, h], y_part, j)

    def y_arrival(s):
        for way, near, inside in ((0, z - 1 - s, z - 1 - s >= 0), (1, z + 1 + s, z + 1 + s <= H - 1)):
            @pl.when(inside)
            def _():
                for h in range(parts):
                    arrive(piece(near, 1 - y, h), gy_send.at[way, s, h], gy_recv.at[way, s, h])
                message_pair(near)

    densify(0, row_blocks // 2)
    z_arrival(0)
    densify(row_blocks // 2, row_blocks)
    if H > 2:
        z_arrival(1)
    loads[2].wait()
    loads[3].wait()
    for f in range(nf):
        cols = slice(f * tile, (f + 1) * tile)
        self_term[:, cols] = dot(paper[...], w_self[:, cols])
    loads[1].wait()
    loads[4].wait()
    for h in range(parts):
        arrive(piece(z, 1 - y, h), gy_send.at[2, 0, h], gy_recv.at[2, 0, h])
    message_pair(z)
    for s in range(2, H - 1):
        z_arrival(s)
        y_arrival(s - 2)
    for s in range(max(H - 3, 0), H - 1):
        y_arrival(s)

    def first_hop(q, f):
        cols = slice(f * tile, (f + 1) * tile)
        return dot(dense[q], msgs[:, :, :, cols].reshape(2 * authors, tile))

    for d in range(1, G + 1):
        b = lax.rem(x + d, G)
        for f in range(nf):
            pair_out[d - 1, f] = first_hop(b * 2 + 1 - c, f).astype(BF16)
            send(None, pair_out.at[d - 1, f], pair_in.at[d - 1, f], pair_s.at[d - 1, f], pair_r.at[d - 1, f], i, c_part)
        for f in range(nf):
            acc[f] = first_hop(b * 2 + c, f)
            arrive(pair_in.at[d - 1, f], pair_s.at[d - 1, f], pair_r.at[d - 1, f])
            acc[f] = acc[f] + pair_in[d - 1, f].astype(F32)
            if d == G:
                continue
            is_up, is_down = b > x, b < x

            @pl.when(is_up & (x > 0))
            def _():
                arrive(x_in.at[0, b, f], xs.at[0, b, f], xr.at[0, b, f])
                acc[f] = acc[f] + x_in[0, b, f].astype(F32)

            @pl.when(is_down & (x < G - 1))
            def _():
                arrive(x_in.at[1, b, f], xs.at[1, b, f], xr.at[1, b, f])
                acc[f] = acc[f] + x_in[1, b, f].astype(F32)

            x_out[d - 1, f] = acc[f].astype(BF16)
            send(is_up, x_out.at[d - 1, f], x_in.at[0, b, f], xs.at[0, b, f], xr.at[0, b, f], i, j + 2)
            send(is_down, x_out.at[d - 1, f], x_in.at[1, b, f], xs.at[1, b, f], xr.at[1, b, f], i, j - 2)

    for f in range(nf):
        cols = slice(f * tile, (f + 1) * tile)

        @pl.when(x > 0)
        def _():
            arrive(x_in.at[0, x, f], xs.at[0, x, f], xr.at[0, x, f])
            acc[f] = acc[f] + x_in[0, x, f].astype(F32)

        @pl.when(x < G - 1)
        def _():
            arrive(x_in.at[1, x, f], xs.at[1, x, f], xr.at[1, x, f])
            acc[f] = acc[f] + x_in[1, x, f].astype(F32)

        hidden[:, cols] = jnp.maximum(acc[f] + self_term[:, cols], 0.0).astype(BF16)

    for f in range(nf):
        cols = slice(f * tile, (f + 1) * tile)
        rows_all[f, x, c] = dot(hidden[...], w_two[:, cols]).astype(BF16)
        own = rows_all.at[f, x, c]
        send(up_x, own, own, o_send.at[0, 0, f], o_recv.at[0, 0, f], i, j + 2)
        send(down_x, own, own, o_send.at[1, 0, f], o_recv.at[1, 0, f], i, j - 2)
        send(None, own, own, oc_send.at[2, 0, f], oc_recv.at[2, 0, f], i, c_part)

    def pass_on(f):
        for s in range(G - 1):
            below, above = x - 1 - s, x + 1 + s

            @pl.when(below >= 0)
            def _():
                arrive(rows_all.at[f, below, c], o_send.at[0, s, f], o_recv.at[0, s, f])

            part = rows_all.at[f, below, c]
            if s + 1 <= G - 2:
                send((below >= 0) & up_x, part, part, o_send.at[0, s + 1, f], o_recv.at[0, s + 1, f], i, j + 2)
            send(below >= 0, part, part, oc_send.at[0, s, f], oc_recv.at[0, s, f], i, c_part)

            @pl.when(above <= G - 1)
            def _():
                arrive(rows_all.at[f, above, c], o_send.at[1, s, f], o_recv.at[1, s, f])

            part = rows_all.at[f, above, c]
            if s + 1 <= G - 2:
                send((above <= G - 1) & down_x, part, part, o_send.at[1, s + 1, f], o_recv.at[1, s + 1, f], i, j - 2)
            send(above <= G - 1, part, part, oc_send.at[1, s, f], oc_recv.at[1, s, f], i, c_part)

    def collect(f):
        arrive(rows_all.at[f, x, 1 - c], oc_send.at[2, 0, f], oc_recv.at[2, 0, f])
        for s in range(G - 1):
            below, above = x - 1 - s, x + 1 + s

            @pl.when(below >= 0)
            def _():
                arrive(rows_all.at[f, below, 1 - c], oc_send.at[0, s, f], oc_recv.at[0, s, f])

            @pl.when(above <= G - 1)
            def _():
                arrive(rows_all.at[f, above, 1 - c], oc_send.at[1, s, f], oc_recv.at[1, s, f])

    for f in range(nf):
        pass_on(f)
        collect(f)
        table = rows_all[f].reshape(papers, tile)
        far = dot(dense_t[1 - y].reshape(H * own_authors, papers), table)
        y_out[f] = far.astype(BF16).reshape(H, own_authors, tile)
        for s in range(H - 1):
            for b, cond in ((H - 1 - s, z < H - 1 - s), (s, z > s)):
                send(cond, y_out.at[f, b], y_in.at[f, b], ys.at[f, b], yr.at[f, b], y_part, j)
        near = dot(dense_t[y].reshape(H * own_authors, papers), table)
        y_acc[f] = near.reshape(H, own_authors, tile)
    for f in range(nf):
        send(None, y_out.at[f, z], y_in.at[f, z], ys.at[f, z], yr.at[f, z], y_part, j)

    for f in range(nf):
        for s in range(H - 1):
            for way, b in ((0, H - 1 - s), (1, s)):
                cond = (z < b) if way == 0 else (z > b)
                first = (z == 0) if way == 0 else (z == H - 1)

                @pl.when(cond)
                def _():
                    arrive(y_in.at[f, b], ys.at[f, b], yr.at[f, b])
                    y_acc[f, b] = y_acc[f, b] + y_in[f, b].astype(F32)

                @pl.when(cond & jnp.logical_not(first))
                def _():
                    arrive(z_in.at[way, f, b], zs.at[way, f, b], zr.at[way, f, b])
                    y_acc[f, b] = y_acc[f, b] + z_in[way, f, b].astype(F32)

                @pl.when(cond)
                def _():
                    z_out[way, f, b] = y_acc[f, b].astype(BF16)

                send(cond, z_out.at[way, f, b], z_in.at[way, f, b], zs.at[way, f, b], zr.at[way, f, b],
                     i + 2 if way == 0 else i - 2, j)

    for f in range(nf):
        cols = slice(f * tile, (f + 1) * tile)
        total = y_acc.at[f, z]
        arrive(y_in.at[f, z], ys.at[f, z], yr.at[f, z])
        total[...] = total[...] + y_in[f, z].astype(F32)

        @pl.when(z > 0)
        def _():
            arrive(z_in.at[0, f, z], zs.at[0, f, z], zr.at[0, f, z])
            total[...] = total[...] + z_in[0, f, z].astype(F32)

        @pl.when(z < H - 1)
        def _():
            arrive(z_in.at[1, f, z], zs.at[1, f, z], zr.at[1, f, z])
            total[...] = total[...] + z_in[1, f, z].astype(F32)

        author_out[:, cols] = total[...].astype(BF16)

    for cond, desc in waits:
        if cond is None:
            desc().wait_send()
        else:
            @pl.when(cond)
            def _():
                desc().wait_send()


def per_device(
    n_prow, n_pcol, paper_x, author_x, w_self, w_rel, w_two,
    block_rows, block_cols, block_type, block_count, block_vals,
):
    slots, side = block_vals.shape[2], block_vals.shape[3]
    own_papers, width = paper_x.shape
    own_authors = author_x.shape[0]
    papers, authors = own_papers * n_pcol, own_authors * n_prow
    col_blocks = authors // side
    places = (papers // side) * col_blocks
    H, G = n_prow // 2, n_pcol // 2
    tile = 256 if width % 256 == 0 else 128
    nf = width // tile

    slot = jnp.arange(slots, dtype=jnp.int32)
    where = block_rows.reshape(slots) * col_blocks + block_cols.reshape(slots)
    live = slot < block_count.reshape(())
    hit = (where[:, None] == jnp.arange(places, dtype=jnp.int32)[None, :]) & live[:, None]
    which = jnp.sum(jnp.where(hit, slot[:, None], 0), axis=0)
    kind = 2 + jnp.sum(jnp.where(hit, block_type.reshape(slots)[:, None] - 2, 0), axis=0)
    tab = jnp.stack([which, kind]).astype(jnp.int32)

    vmem, anyspace, smem = pltpu.VMEM, pl.ANY, pltpu.SMEM
    dma = pltpu.SemaphoreType.DMA
    hz, gx = max(H - 1, 1), max(G - 1, 1)
    return pl.pallas_call(
        functools.partial(kernel, n_prow, n_pcol, tile),
        out_shape=(
            jax.ShapeDtypeStruct((own_papers, width), BF16),
            jax.ShapeDtypeStruct((own_authors, width), BF16),
        ),
        in_specs=[pl.BlockSpec(memory_space=smem), pl.BlockSpec(memory_space=vmem)]
        + [pl.BlockSpec(memory_space=anyspace)] * 5,
        out_specs=(pl.BlockSpec(memory_space=vmem),) * 2,
        scratch_shapes=[
            vmem((own_papers, width), BF16),
            vmem((width, width), BF16),
            vmem(w_rel.shape, BF16),
            vmem((width, width), BF16),
            vmem((slots, side, side), BF16),
            vmem((H, 2, own_authors, width), BF16),
            vmem((2, H, 2 * own_authors, width), BF16),
            vmem((n_pcol, own_papers, 2 * authors), BF16),
            vmem((2, H, own_authors, papers), BF16),
            vmem((own_papers, width), F32),
            vmem((G, nf, own_papers, tile), BF16),
            vmem((G, nf, own_papers, tile), BF16),
            vmem((gx, nf, own_papers, tile), BF16),
            vmem((2, G, nf, own_papers, tile), BF16),
            vmem((nf, own_papers, tile), F32),
            vmem((nf, G, 2, own_papers, tile), BF16),
            vmem((nf, H, own_authors, tile), BF16),
            vmem((nf, H, own_authors, tile), BF16),
            vmem((nf, H, own_authors, tile), F32),
            vmem((2, nf, H, own_authors, tile), BF16),
            vmem((2, nf, H, own_authors, tile), BF16),
            dma((5,)),
            dma((2, hz, 2)), dma((2, hz, 2)), dma((3, hz, 2)), dma((3, hz, 2)),
            dma((G, nf)), dma((G, nf)), dma((2, G, nf)), dma((2, G, nf)),
            dma((2, gx, nf)), dma((2, gx, nf)), dma((3, gx, nf)), dma((3, gx, nf)),
            dma((nf, H)), dma((nf, H)), dma((2, nf, H)), dma((2, nf, H)),
        ],
        compiler_params=pltpu.CompilerParams(
            collective_id=0, has_side_effects=True, vmem_limit_bytes=60 * 1024 * 1024
        ),
    )(tab, author_x, paper_x, w_self, w_rel, w_two, block_vals.reshape(slots, side, side))


def solution(mesh):
    return jax.shard_map(
        functools.partial(per_device, mesh.shape["prow"], mesh.shape["pcol"]),
        mesh=mesh,
        in_specs=(
            P(("prow", "pcol"), None),
            P(("pcol", "prow"), None),
            P(),
            P(),
            P(),
            P("prow", "pcol", None),
            P("prow", "pcol", None),
            P("prow", "pcol", None),
            P("prow", "pcol"),
            P("prow", "pcol", None, None, None),
        ),
        out_specs=(P(("prow", "pcol"), None), P(("pcol", "prow"), None)),
        check_vma=False,
    )
```

```python
import functools

import jax
import jax.numpy as jnp
from jax import lax
from jax.experimental import pallas as pl
from jax.experimental.pallas import tpu as pltpu
from jax.sharding import PartitionSpec as P

MESH = pl.DeviceIdType.MESH
F32 = jnp.float32
BF16 = jnp.bfloat16


def dot(a, b):
    return jnp.dot(a, b, preferred_element_type=F32)


def kernel(
    n_prow, n_pcol, tile,
    tab, author, paper_h, w_self_h, w_rel_h, w_two_h, blocks_h,
    hidden, author_out,
    paper, w_self, w_rel, w_two, blocks,
    x_all, msgs, dense, dense_t, self_term,
    pair_out, pair_in, x_out, x_in, acc,
    rows_all, y_out, y_in, y_acc, z_out, z_in,
    local_sem,
    g_send, g_recv, gy_send, gy_recv,
    pair_s, pair_r, xs, xr,
    o_send, o_recv, oc_send, oc_recv,
    ys, yr, zs, zr,
):
    i = lax.axis_index("prow")
    j = lax.axis_index("pcol")
    z, y = i // 2, i % 2
    x, c = j // 2, j % 2
    H, G = n_prow // 2, n_pcol // 2
    own_papers, width = paper.shape
    own_authors = author.shape[0]
    side = blocks.shape[1]
    authors = own_authors * n_prow
    papers = own_papers * n_pcol
    nf = width // tile
    y_part = z * 2 + 1 - y
    c_part = x * 2 + 1 - c

    waits = []

    def send(cond, src, dst, ss, rs, di, dj):
        def desc():
            return pltpu.make_async_remote_copy(
                src_ref=src, dst_ref=dst, send_sem=ss, recv_sem=rs,
                device_id=(di, dj), device_id_type=MESH,
            )

        if cond is None:
            desc().start()
        else:
            @pl.when(cond)
            def _():
                desc().start()
        waits.append((cond, desc))

    def arrive(dst, ss, rs):
        pltpu.make_async_remote_copy(
            src_ref=dst, dst_ref=dst, send_sem=ss, recv_sem=rs,
            device_id=(i, c_part), device_id_type=MESH,
        ).wait_recv()

    loads = [
        pltpu.make_async_copy(src, dst, local_sem.at[n])
        for n, (src, dst) in enumerate(
            ((blocks_h, blocks), (w_rel_h, w_rel), (paper_h, paper), (w_self_h, w_self), (w_two_h, w_two))
        )
    ]
    for load in loads:
        load.start()

    barrier = pltpu.get_barrier_semaphore()

    def greet(cond, di, dj):
        def go():
            pl.semaphore_signal(barrier, inc=1, device_id=(di, dj), device_id_type=MESH)

        if cond is None:
            go()
        else:
            pl.when(cond)(go)

    up_z, down_z, up_x, down_x = z < H - 1, z > 0, x < G - 1, x > 0
    greet(None, y_part, j)
    greet(None, i, c_part)
    greet(up_z, i + 2, j)
    greet(down_z, i - 2, j)
    greet(up_x, i, j + 2)
    greet(down_x, i, j - 2)
    peers = 2
    for cond in (up_z, down_z, up_x, down_x):
        peers = peers + cond.astype(jnp.int32)
    pl.semaphore_wait(barrier, peers)

    parts = g_send.shape[2]
    part_rows = own_authors // parts

    def piece(zz, yy, h):
        return x_all.at[zz, yy, pl.ds(h * part_rows, part_rows), :]

    for h in range(parts):
        mine = author.at[pl.ds(h * part_rows, part_rows), :]
        send(up_z, mine, piece(z, y, h), g_send.at[0, 0, h], g_recv.at[0, 0, h], i + 2, j)
        send(down_z, mine, piece(z, y, h), g_send.at[1, 0, h], g_recv.at[1, 0, h], i - 2, j)
        send(None, mine, piece(z, y, h), gy_send.at[2, 0, h], gy_recv.at[2, 0, h], y_part, j)
    x_all[z, y] = author[...]

    loads[0].wait()
    row_blocks, col_blocks = papers // side, authors // side
    p_step, a_step = min(side, own_papers), min(side, own_authors)

    def densify(first, last):
        for rb in range(first, last):
            for cb in range(col_blocks):
                pos = rb * col_blocks + cb
                slot, kind = tab[0, pos], tab[1, pos]
                block = blocks[slot].astype(F32)
                for t in range(2):
                    part = (block * (kind == t).astype(F32)).astype(BF16)
                    lo = t * authors + cb * side
                    for sub in range(side // p_step):
                        row = rb * side + sub * p_step
                        dense[row // own_papers, row % own_papers:row % own_papers + p_step, lo:lo + side] = part[
                            sub * p_step:(sub + 1) * p_step
                        ]
                flip = (block * (kind < 2).astype(F32)).T.astype(BF16)
                for sub in range(side // a_step):
                    owner = (cb * side + sub * a_step) // own_authors
                    dense_t[owner % 2, owner // 2, :, rb * side:(rb + 1) * side] = flip[sub * a_step:(sub + 1) * a_step]

    def message_pair(zz):
        pair = x_all[zz].reshape(2 * own_authors, width)
        for t in range(2):
            @pl.loop(0, nf)
            def _(n):
                cols = pl.ds(pl.multiple_of(n * tile, tile), tile)
                msgs[t, zz, :, cols] = dot(pair, w_rel[t, :, cols]).astype(BF16)

    def z_arrival(s):
        for h in range(parts):
            for way, near, inside, more, to in (
                (0, z - 1 - s, z - 1 - s >= 0, up_z, i + 2),
                (1, z + 1 + s, z + 1 + s <= H - 1, down_z, i - 2),
            ):
                part = piece(near, y, h)

                @pl.when(inside)
                def _():
                    arrive(part, g_send.at[way, s, h], g_recv.at[way, s, h])

                if s + 1 <= H - 2:
                    send(inside & more, part, part, g_send.at[way, s + 1, h], g_recv.at[way, s + 1, h], to, j)
                send(inside, part, part, gy_send.at[way, s, h], gy_recv.at[way, s, h], y_part, j)

    def y_arrival(s):
        for way, near, inside in ((0, z - 1 - s, z - 1 - s >= 0), (1, z + 1 + s, z + 1 + s <= H - 1)):
            @pl.when(inside)
            def _():
                for h in range(parts):
                    arrive(piece(near, 1 - y, h), gy_send.at[way, s, h], gy_recv.at[way, s, h])
                message_pair(near)

    densify(0, row_blocks // 2)
    z_arrival(0)
    densify(row_blocks // 2, row_blocks)
    if H > 2:
        z_arrival(1)
    loads[2].wait()
    loads[3].wait()
    for f in range(nf):
        cols = slice(f * tile, (f + 1) * tile)
        self_term[:, cols] = dot(paper[...], w_self[:, cols])
    loads[1].wait()
    loads[4].wait()
    for h in range(parts):
        arrive(piece(z, 1 - y, h), gy_send.at[2, 0, h], gy_recv.at[2, 0, h])
    message_pair(z)
    for s in range(2, H - 1):
        z_arrival(s)
        y_arrival(s - 2)
    for s in range(max(H - 3, 0), H - 1):
        y_arrival(s)

    def first_hop(q, f):
        cols = slice(f * tile, (f + 1) * tile)
        return dot(dense[q], msgs[:, :, :, cols].reshape(2 * authors, tile))

    for d in range(1, G + 1):
        b = lax.rem(x + d, G)
        for f in range(nf):
            pair_out[d - 1, f] = first_hop(b * 2 + 1 - c, f).astype(BF16)
            send(None, pair_out.at[d - 1, f], pair_in.at[d - 1, f], pair_s.at[d - 1, f], pair_r.at[d - 1, f], i, c_part)
        for f in range(nf):
            acc[f] = first_hop(b * 2 + c, f)
            arrive(pair_in.at[d - 1, f], pair_s.at[d - 1, f], pair_r.at[d - 1, f])
            acc[f] = acc[f] + pair_in[d - 1, f].astype(F32)
            if d == G:
                continue
            is_up, is_down = b > x, b < x

            @pl.when(is_up & (x > 0))
            def _():
                arrive(x_in.at[0, b, f], xs.at[0, b, f], xr.at[0, b, f])
                acc[f] = acc[f] + x_in[0, b, f].astype(F32)

            @pl.when(is_down & (x < G - 1))
            def _():
                arrive(x_in.at[1, b, f], xs.at[1, b, f], xr.at[1, b, f])
                acc[f] = acc[f] + x_in[1, b, f].astype(F32)

            x_out[d - 1, f] = acc[f].astype(BF16)
            send(is_up, x_out.at[d - 1, f], x_in.at[0, b, f], xs.at[0, b, f], xr.at[0, b, f], i, j + 2)
            send(is_down, x_out.at[d - 1, f], x_in.at[1, b, f], xs.at[1, b, f], xr.at[1, b, f], i, j - 2)

    for f in range(nf):
        cols = slice(f * tile, (f + 1) * tile)

        @pl.when(x > 0)
        def _():
            arrive(x_in.at[0, x, f], xs.at[0, x, f], xr.at[0, x, f])
            acc[f] = acc[f] + x_in[0, x, f].astype(F32)

        @pl.when(x < G - 1)
        def _():
            arrive(x_in.at[1, x, f], xs.at[1, x, f], xr.at[1, x, f])
            acc[f] = acc[f] + x_in[1, x, f].astype(F32)

        hidden[:, cols] = jnp.maximum(acc[f] + self_term[:, cols], 0.0).astype(BF16)

    for f in range(nf):
        cols = slice(f * tile, (f + 1) * tile)
        rows_all[f, x, c] = dot(hidden[...], w_two[:, cols]).astype(BF16)
        own = rows_all.at[f, x, c]
        send(up_x, own, own, o_send.at[0, 0, f], o_recv.at[0, 0, f], i, j + 2)
        send(down_x, own, own, o_send.at[1, 0, f], o_recv.at[1, 0, f], i, j - 2)
        send(None, own, own, oc_send.at[2, 0, f], oc_recv.at[2, 0, f], i, c_part)

    def pass_on(f):
        for s in range(G - 1):
            below, above = x - 1 - s, x + 1 + s

            @pl.when(below >= 0)
            def _():
                arrive(rows_all.at[f, below, c], o_send.at[0, s, f], o_recv.at[0, s, f])

            part = rows_all.at[f, below, c]
            if s + 1 <= G - 2:
                send((below >= 0) & up_x, part, part, o_send.at[0, s + 1, f], o_recv.at[0, s + 1, f], i, j + 2)
            send(below >= 0, part, part, oc_send.at[0, s, f], oc_recv.at[0, s, f], i, c_part)

            @pl.when(above <= G - 1)
            def _():
                arrive(rows_all.at[f, above, c], o_send.at[1, s, f], o_recv.at[1, s, f])

            part = rows_all.at[f, above, c]
            if s + 1 <= G - 2:
                send((above <= G - 1) & down_x, part, part, o_send.at[1, s + 1, f], o_recv.at[1, s + 1, f], i, j - 2)
            send(above <= G - 1, part, part, oc_send.at[1, s, f], oc_recv.at[1, s, f], i, c_part)

    def collect(f):
        arrive(rows_all.at[f, x, 1 - c], oc_send.at[2, 0, f], oc_recv.at[2, 0, f])
        for s in range(G - 1):
            below, above = x - 1 - s, x + 1 + s

            @pl.when(below >= 0)
            def _():
                arrive(rows_all.at[f, below, 1 - c], oc_send.at[0, s, f], oc_recv.at[0, s, f])

            @pl.when(above <= G - 1)
            def _():
                arrive(rows_all.at[f, above, 1 - c], oc_send.at[1, s, f], oc_recv.at[1, s, f])

    low = z < H // 2
    for f in range(nf):
        pass_on(f)
        collect(f)
        table = rows_all[f].reshape(papers, tile)
        far = dot(dense_t[1 - y].reshape(H * own_authors, papers), table)
        y_out[f] = far.astype(BF16).reshape(H, own_authors, tile)
        for s in range(H - 1):
            for b, cond in ((H - 1 - s, (z < H - 1 - s) & low), (s, z > s), (H - 1 - s, (z < H - 1 - s) & (z >= H // 2))):
                send(cond, y_out.at[f, b], y_in.at[f, b], ys.at[f, b], yr.at[f, b], y_part, j)
        near = dot(dense_t[y].reshape(H * own_authors, papers), table)
        y_acc[f] = near.reshape(H, own_authors, tile)
    for f in range(nf):
        send(None, y_out.at[f, z], y_in.at[f, z], ys.at[f, z], yr.at[f, z], y_part, j)

    for f in range(nf):
        for s in range(H - 1):
            for way, b, cond in (
                (0, H - 1 - s, (z < H - 1 - s) & low), (1, s, z > s), (0, H - 1 - s, (z < H - 1 - s) & (z >= H // 2))
            ):
                first = (z == 0) if way == 0 else (z == H - 1)

                @pl.when(cond)
                def _():
                    arrive(y_in.at[f, b], ys.at[f, b], yr.at[f, b])
                    y_acc[f, b] = y_acc[f, b] + y_in[f, b].astype(F32)

                @pl.when(cond & jnp.logical_not(first))
                def _():
                    arrive(z_in.at[way, f, b], zs.at[way, f, b], zr.at[way, f, b])
                    y_acc[f, b] = y_acc[f, b] + z_in[way, f, b].astype(F32)

                @pl.when(cond)
                def _():
                    z_out[way, f, b] = y_acc[f, b].astype(BF16)

                send(cond, z_out.at[way, f, b], z_in.at[way, f, b], zs.at[way, f, b], zr.at[way, f, b],
                     i + 2 if way == 0 else i - 2, j)

    for f in range(nf):
        cols = slice(f * tile, (f + 1) * tile)
        total = y_acc.at[f, z]
        arrive(y_in.at[f, z], ys.at[f, z], yr.at[f, z])
        total[...] = total[...] + y_in[f, z].astype(F32)

        @pl.when(z > 0)
        def _():
            arrive(z_in.at[0, f, z], zs.at[0, f, z], zr.at[0, f, z])
            total[...] = total[...] + z_in[0, f, z].astype(F32)

        @pl.when(z < H - 1)
        def _():
            arrive(z_in.at[1, f, z], zs.at[1, f, z], zr.at[1, f, z])
            total[...] = total[...] + z_in[1, f, z].astype(F32)

        author_out[:, cols] = total[...].astype(BF16)

    for cond, desc in waits:
        if cond is None:
            desc().wait_send()
        else:
            @pl.when(cond)
            def _():
                desc().wait_send()


def per_device(
    n_prow, n_pcol, paper_x, author_x, w_self, w_rel, w_two,
    block_rows, block_cols, block_type, block_count, block_vals,
):
    slots, side = block_vals.shape[2], block_vals.shape[3]
    own_papers, width = paper_x.shape
    own_authors = author_x.shape[0]
    papers, authors = own_papers * n_pcol, own_authors * n_prow
    col_blocks = authors // side
    places = (papers // side) * col_blocks
    H, G = n_prow // 2, n_pcol // 2
    tile = 256 if width % 256 == 0 else 128
    nf = width // tile

    slot = jnp.arange(slots, dtype=jnp.int32)
    where = block_rows.reshape(slots) * col_blocks + block_cols.reshape(slots)
    live = slot < block_count.reshape(())
    hit = (where[:, None] == jnp.arange(places, dtype=jnp.int32)[None, :]) & live[:, None]
    which = jnp.sum(jnp.where(hit, slot[:, None], 0), axis=0)
    kind = 2 + jnp.sum(jnp.where(hit, block_type.reshape(slots)[:, None] - 2, 0), axis=0)
    tab = jnp.stack([which, kind]).astype(jnp.int32)

    vmem, anyspace, smem = pltpu.VMEM, pl.ANY, pltpu.SMEM
    dma = pltpu.SemaphoreType.DMA
    hz, gx = max(H - 1, 1), max(G - 1, 1)
    return pl.pallas_call(
        functools.partial(kernel, n_prow, n_pcol, tile),
        out_shape=(
            jax.ShapeDtypeStruct((own_papers, width), BF16),
            jax.ShapeDtypeStruct((own_authors, width), BF16),
        ),
        in_specs=[pl.BlockSpec(memory_space=smem), pl.BlockSpec(memory_space=vmem)]
        + [pl.BlockSpec(memory_space=anyspace)] * 5,
        out_specs=(pl.BlockSpec(memory_space=vmem),) * 2,
        scratch_shapes=[
            vmem((own_papers, width), BF16),
            vmem((width, width), BF16),
            vmem(w_rel.shape, BF16),
            vmem((width, width), BF16),
            vmem((slots, side, side), BF16),
            vmem((H, 2, own_authors, width), BF16),
            vmem((2, H, 2 * own_authors, width), BF16),
            vmem((n_pcol, own_papers, 2 * authors), BF16),
            vmem((2, H, own_authors, papers), BF16),
            vmem((own_papers, width), F32),
            vmem((G, nf, own_papers, tile), BF16),
            vmem((G, nf, own_papers, tile), BF16),
            vmem((gx, nf, own_papers, tile), BF16),
            vmem((2, G, nf, own_papers, tile), BF16),
            vmem((nf, own_papers, tile), F32),
            vmem((nf, G, 2, own_papers, tile), BF16),
            vmem((nf, H, own_authors, tile), BF16),
            vmem((nf, H, own_authors, tile), BF16),
            vmem((nf, H, own_authors, tile), F32),
            vmem((2, nf, H, own_authors, tile), BF16),
            vmem((2, nf, H, own_authors, tile), BF16),
            dma((5,)),
            dma((2, hz, 2)), dma((2, hz, 2)), dma((3, hz, 2)), dma((3, hz, 2)),
            dma((G, nf)), dma((G, nf)), dma((2, G, nf)), dma((2, G, nf)),
            dma((2, gx, nf)), dma((2, gx, nf)), dma((3, gx, nf)), dma((3, gx, nf)),
            dma((nf, H)), dma((nf, H)), dma((2, nf, H)), dma((2, nf, H)),
        ],
        compiler_params=pltpu.CompilerParams(
            collective_id=0, has_side_effects=True, vmem_limit_bytes=60 * 1024 * 1024
        ),
    )(tab, author_x, paper_x, w_self, w_rel, w_two, block_vals.reshape(slots, side, side))


def solution(mesh):
    return jax.shard_map(
        functools.partial(per_device, mesh.shape["prow"], mesh.shape["pcol"]),
        mesh=mesh,
        in_specs=(
            P(("prow", "pcol"), None),
            P(("pcol", "prow"), None),
            P(),
            P(),
            P(),
            P("prow", "pcol", None),
            P("prow", "pcol", None),
            P("prow", "pcol", None),
            P("prow", "pcol"),
            P("prow", "pcol", None, None, None),
        ),
        out_specs=(P(("prow", "pcol"), None), P(("pcol", "prow"), None)),
        check_vma=False,
    )
```
